32 devices in a mesh: expert: 8 (over z, core), tensor: 4 (over y, x).
Axes of the slice: x: 2, y: 2, z: 4, core: 2. Of those that a mesh axis runs over, the one named last changes fastest.
Arguments:
- residual_in: bfloat16 [1024, 3584], P('expert'), may hold values from -8 to 8
- head_outputs: bfloat16 [1024, 4096], P('expert', 'tensor'), may hold values from -6 to 6
- out_weight: bfloat16 [4096, 3584], P('tensor'), may hold values from -0.09375 to 0.09375
- gain_in: float32 [3584], replicated, may hold values from 0.25 to 1.75
- dense_gate: bfloat16 [3584, 2432], P(None, 'tensor'), may hold values from -0.09375 to 0.09375
- dense_up: bfloat16 [3584, 2432], P(None, 'tensor'), may hold values from -0.09375 to 0.09375
- dense_down: bfloat16 [2432, 3584], P('tensor'), may hold values from -0.125 to 0.125
- expert_ids: int32 [1024, 2], P('expert'), may hold values from 0 to 7, all different within a row
- route_weights: float32 [1024, 2], P('expert'), may hold values from 0.1 to 1
- gain_moe: float32 [3584], replicated, may hold values from 0.25 to 1.75
- expert_gate: bfloat16 [8, 3584, 2432], P('expert', None, 'tensor'), may hold values from -0.09375 to 0.09375
- expert_up: bfloat16 [8, 3584, 2432], P('expert', None, 'tensor'), may hold values from -0.09375 to 0.09375
- expert_down: bfloat16 [8, 2432, 3584], P('expert', 'tensor'), may hold values from -0.125 to 0.125
Outputs:
- layer_out: bfloat16 [1024, 3584], P('expert', 'tensor')
The draws below stay inside these ranges and needn't reach their ends.
Inputs may be any that keep to these rules, and one draw needn't show every extreme that they name: `expert_ids`: each row names two different experts.
All inputs are finite; a program needn't handle non-finite values.
Results may differ from the reference program's by a relative error of at most 0.006.
Values may be sent and summed in bfloat16 or wider, within the bound.
No kernel may reach another device: no remote copies, remote signals or barrier semaphores. Data moves between devices by JAX's collectives and lax.ppermute only.
A program may use at most 64 MiB of HBM per device.

```python
import jax
import jax.numpy as jnp
from jax import lax

D = 3584
HEADS = 32
HEAD_DIM = 128
FF_DENSE = 2432
FF_EXP = 2432
TOK_DEV = 128
EXPERTS = 8
CAP = 32
TOKENS = 1024


def draw_residual_in(key, part):
    columns = jnp.arange(D, dtype=jnp.float32) / (D - 1)
    base = jax.random.truncated_normal(key, -4.0, 4.0, (TOKENS, D), jnp.float32)
    scales = 0.6 + 1.2 * columns
    return (base * scales[None, :]).astype(jnp.bfloat16)


def levels(stream_key, dims, cuts, low, largest):
    def one(dim, parts):
        draws = jax.random.uniform(jax.random.fold_in(jax.random.fold_in(stream_key, 6), dim), (parts,), jnp.float32, low / len(cuts), largest / len(cuts))
        return jnp.repeat(jnp.exp(draws), dims[dim] // parts).reshape((-1,) + (1,) * (len(dims) - dim - 1))

    level = one(*cuts[0])
    for cut in cuts[1:]:
        level = level * one(*cut)
    return level


def choose_distinct(rng, rows, amount, top, lift):
    order = jax.random.permutation(jax.random.fold_in(rng, 1), amount)
    boost = order
    for power in range(3):
        boost = boost * boost // amount
    boost = boost * lift // amount
    lots = jax.random.randint(jax.random.fold_in(rng, 2), (rows, amount), 0, 4096) + boost
    fixed_rows = jax.random.permutation(jax.random.fold_in(rng, 3), rows)[jnp.arange(amount) % rows]
    lots = jnp.where(jnp.arange(rows)[:, None] == fixed_rows[None, :], 1 << 14, lots)
    merit = lots * amount + jnp.arange(amount)
    return lax.top_k(merit.astype(jnp.int32), top)[1].astype(jnp.int32)


def bell_draw(rng, dims, width, most, pieces=(), kind=jnp.bfloat16):
    array = jax.random.normal(rng, dims, jnp.float32) * width
    if len(pieces) > 0:
        array = levels(rng, dims, pieces, -0.22, 0.18) * array
    return jnp.clip(array, min=-most, max=most).astype(kind)


def setup_inputs(seed: int = 0) -> dict:
    splits = jax.random.split(jax.random.key(seed), 14)
    return {
        "residual_in": draw_residual_in(jax.random.fold_in(splits[13], 71), 0),
        "head_outputs": bell_draw(splits[1], (TOKENS, HEADS * HEAD_DIM), 1.0, 6.0, ((0, 8), (1, 4))),
        "out_weight": bell_draw(splits[2], (HEADS * HEAD_DIM, D), (HEADS * HEAD_DIM) ** -0.5, 0.09375, ((0, 4),)),
        "gain_in": jnp.clip(1.0 + 0.15 * jax.random.normal(splits[3], (D,), jnp.float32), 0.25, 1.75),
        "dense_gate": bell_draw(splits[4], (D, FF_DENSE), D ** -0.5, 0.09375, ((1, 4),)),
        "dense_up": bell_draw(splits[5], (D, FF_DENSE), D ** -0.5, 0.09375, ((1, 4),)),
        "dense_down": bell_draw(splits[6], (FF_DENSE, D), FF_DENSE ** -0.5, 0.125, ((0, 4),)),
        "expert_ids": choose_distinct(splits[7], TOKENS, EXPERTS, 2, 4096),
        "route_weights": jnp.clip(0.1 + 0.9 * jax.random.uniform(splits[8], (TOKENS, 2), jnp.float32) ** levels(splits[8], (TOKENS, 2), ((0, 8),), -0.2, 0.2), 0.1, 1.0),
        "gain_moe": jnp.clip(1.0 + 0.15 * jax.random.normal(splits[9], (D,), jnp.float32), 0.25, 1.75),
        "expert_gate": bell_draw(splits[10], (EXPERTS, D, FF_EXP), D ** -0.5, 0.09375, ((0, 8), (2, 4))),
        "expert_up": bell_draw(splits[11], (EXPERTS, D, FF_EXP), D ** -0.5, 0.09375, ((0, 8), (2, 4))),
        "expert_down": bell_draw(splits[12], (EXPERTS, FF_EXP, D), FF_EXP ** -0.5, 0.125, ((0, 8), (1, 4))),
    }


eps = 1e-05

def rms_norm(values, gain):
    return values * lax.rsqrt(lax.optimization_barrier(jnp.mean(values * values, axis=-1, keepdims=True)) + eps) * gain

def reference(residual_in, head_outputs, out_weight, gain_in, dense_gate, dense_up, dense_down, expert_ids, route_weights, gain_moe, expert_gate, expert_up, expert_down):
    x_float = residual_in.astype(jnp.float32)
    normed = rms_norm(x_float, gain_in).astype(jnp.bfloat16)
    dense_hidden = (jax.nn.silu(jnp.dot(normed, dense_gate, preferred_element_type=jnp.float32)) * jnp.dot(normed, dense_up, preferred_element_type=jnp.float32)).astype(jnp.bfloat16)
    mixed = x_float + (jnp.dot(head_outputs, out_weight, preferred_element_type=jnp.float32) + jnp.dot(dense_hidden, dense_down, preferred_element_type=jnp.float32))
    routed = rms_norm(mixed, gain_moe).astype(jnp.bfloat16)
    groups = TOKENS // TOK_DEV
    assigned = TOK_DEV * 2
    group_ids = expert_ids.reshape(groups, assigned)
    onehot = (group_ids[:, :, None] == jnp.arange(EXPERTS, dtype=jnp.int32)[None, None, :]).astype(jnp.int32)
    earlier = jnp.cumsum(onehot, axis=1) - onehot
    position = lax.optimization_barrier(jnp.sum(earlier * onehot, axis=2)).astype(jnp.int32)
    kept = position < CAP
    group_index = jnp.arange(groups, dtype=jnp.int32)[:, None]
    slot_index = (group_ids * (groups * CAP) + group_index * CAP + position).astype(jnp.int32)
    slot_total = EXPERTS * groups * CAP
    target = jnp.where(kept, slot_index, slot_total + 7).astype(jnp.int32)
    token_index = (group_index * TOK_DEV + jnp.arange(assigned, dtype=jnp.int32)[None, :] // 2).astype(jnp.int32)
    slot_table = jnp.full((slot_total,), TOKENS, jnp.int32).at[target.reshape(-1)].set(token_index.reshape(-1), mode='drop')
    slot_table = slot_table.reshape(EXPERTS, groups * CAP)
    padded = jnp.concatenate([routed, jnp.zeros((1, D), jnp.bfloat16)], axis=0)

    def one_expert(operands):
        row_index, gate_weight, up_weight, down_weight = operands
        slot_rows = padded[row_index]
        gate_sum = jnp.dot(slot_rows, gate_weight, preferred_element_type=jnp.float32)
        up_sum = jnp.dot(slot_rows, up_weight, preferred_element_type=jnp.float32)
        hidden = (jax.nn.silu(gate_sum) * up_sum).astype(jnp.bfloat16)
        return jnp.dot(hidden, down_weight, preferred_element_type=jnp.float32).astype(jnp.bfloat16)
    results = lax.map(one_expert, (slot_table, expert_gate, expert_up, expert_down))
    flat_out = results.reshape(slot_total, D)
    safe_index = jnp.where(kept, slot_index, 0).astype(jnp.int32)
    picked = jnp.where(kept[:, :, None], flat_out[safe_index].astype(jnp.float32), 0.0)
    weights = route_weights.reshape(groups, assigned)
    moe_out = (picked * weights[:, :, None]).reshape(groups, TOK_DEV, 2, D).sum(axis=2).reshape(TOKENS, D)
    return (mixed + moe_out).astype(jnp.bfloat16)
```

```python
import jax
import jax.numpy as jnp
from jax import lax
from jax.sharding import PartitionSpec as P

eps = 1e-05


def exchange(value, axis, flip):
    count = lax.axis_size(axis)
    return lax.ppermute(value, axis, [(i, i ^ flip) for i in range(count)])


def matmul(left, right):
    return jnp.dot(left, right, preferred_element_type=jnp.float32)


def shards(
    residual_in,
    head_outputs,
    out_weight,
    gain_in,
    dense_gate,
    dense_up,
    dense_down,
    expert_ids,
    route_weights,
    gain_moe,
    expert_gate,
    expert_up,
    expert_down,
):
    tok_rows, model_width = residual_in.shape
    experts_count = lax.axis_size("expert")
    tensor_count = lax.axis_size("tensor")
    capacity = 2 * tok_rows // experts_count
    slot_count = experts_count * capacity
    local_cols = model_width // tensor_count
    me_t = lax.axis_index("tensor")
    me_e = lax.axis_index("expert")

    def block(array, flip, axis):
        return lax.dynamic_slice_in_dim(array, (me_t ^ flip) * local_cols, local_cols, axis)

    x_float = residual_in.astype(jnp.float32)
    normed = (
        x_float * lax.rsqrt(jnp.mean(x_float * x_float, axis=1, keepdims=True) + eps) * gain_in
    ).astype(jnp.bfloat16)
    dense_hidden = (
        jax.nn.silu(matmul(normed, dense_gate)) * matmul(normed, dense_up)
    ).astype(jnp.bfloat16)
    partial_value = matmul(head_outputs, out_weight) + matmul(dense_hidden, dense_down)

    chips = experts_count // 2
    flat_ids = expert_ids.reshape(-1)
    onehot = (flat_ids[:, None] == jnp.arange(experts_count, dtype=jnp.int32)[None, :]).astype(
        jnp.int32
    )
    earlier = jnp.cumsum(onehot, axis=0) - onehot
    position = jnp.sum(earlier * onehot, axis=1)
    relative = flat_ids ^ me_e
    order = (relative % 2) * chips + relative // 2
    slot_index = jnp.where(position < capacity, order * capacity + position, -1).reshape(
        tok_rows, 2
    )
    matches = slot_index[:, :, None] == jnp.arange(slot_count, dtype=jnp.int32)[None, None, :]
    placing = jnp.sum(matches.astype(jnp.bfloat16), axis=1)
    weighing = jnp.sum(matches.astype(jnp.float32) * route_weights[:, :, None], axis=1)

    mixed_cols = block(x_float, 0, 1) + block(partial_value, 0, 1)
    for flip in range(1, tensor_count):
        mixed_cols += exchange(
            block(partial_value, flip, 1).astype(jnp.bfloat16), "tensor", flip
        ).astype(jnp.float32)
    gained = (mixed_cols * block(gain_moe, 0, 0)).astype(jnp.bfloat16)
    outgoing = lax.dot_general(
        placing, gained, (((0,), (0,)), ((), ())), preferred_element_type=jnp.float32
    ).astype(jnp.bfloat16)
    half = slot_count // 2
    mine = outgoing[:half].reshape(chips, capacity, local_cols)
    other = exchange(outgoing[half:], "expert", 1).reshape(chips, capacity, local_cols)
    both = jnp.concatenate([mine, other], axis=1)
    received = [both[0]] + [exchange(both[k], "expert", 2 * k) for k in range(1, chips)]
    rows = jnp.concatenate(received, axis=0)
    gate_sum = jnp.zeros((slot_count, expert_gate.shape[2]), jnp.float32)
    up_sum = gate_sum
    squares = jnp.zeros((slot_count, 1), jnp.float32)
    for flip in range(tensor_count):
        piece = rows if flip == 0 else exchange(rows, "tensor", flip)
        gate_sum += matmul(piece, block(expert_gate[0], flip, 0))
        up_sum += matmul(piece, block(expert_up[0], flip, 0))
        plain = piece.astype(jnp.float32) / block(gain_moe, flip, 0)
        squares += jnp.sum(plain * plain, axis=1, keepdims=True)
    scale = lax.rsqrt(squares / model_width + eps)
    hidden = (jax.nn.silu(gate_sum * scale) * (up_sum * scale)).astype(jnp.bfloat16)
    down = expert_down[0]
    result = matmul(hidden, block(down, 0, 1))
    for flip in range(1, tensor_count):
        result += exchange(
            matmul(hidden, block(down, flip, 1)).astype(jnp.bfloat16), "tensor", flip
        ).astype(jnp.float32)
    result = result.astype(jnp.bfloat16).reshape(chips, 2 * capacity, local_cols)
    returned = jnp.stack(
        [result[0]] + [exchange(result[k], "expert", 2 * k) for k in range(1, chips)]
    )
    mine = returned[:, :capacity].reshape(half, local_cols)
    other = exchange(returned[:, capacity:].reshape(half, local_cols), "expert", 1)
    back = jnp.concatenate([mine, other], axis=0)
    moe_out = jnp.dot(weighing, back.astype(jnp.float32), precision=lax.Precision.HIGHEST)
    return (mixed_cols + moe_out).astype(jnp.bfloat16)


def solution(mesh):
    return jax.shard_map(
        shards,
        mesh=mesh,
        in_specs=(
            P("expert", None),
            P("expert", "tensor"),
            P("tensor", None),
            P(),
            P(None, "tensor"),
            P(None, "tensor"),
            P("tensor", None),
            P("expert", None),
            P("expert", None),
            P(),
            P("expert", None, "tensor"),
            P("expert", None, "tensor"),
            P("expert", "tensor", None),
        ),
        out_specs=P("expert", "tensor"),
        check_vma=False,
    )
```
